32 devices in a mesh: rows: 4 (over z), cols: 8 (over y, x, core).
Axes of the slice: x: 2, y: 2, z: 4, core: 2. Of those that a mesh axis runs over, the one named last changes fastest.
Arguments:
- left_query: bfloat16 [8, 1024, 256], P('rows', 'cols'), parts along dimension 0, may hold values from -16 to 16
- left_value: bfloat16 [8, 1024, 256], P('rows', 'cols'), parts along dimension 0, may hold values from -6 to 6
- right_key: bfloat16 [8, 1024, 256], P('rows', 'cols'), parts along dimension 0, may hold values from -16 to 16
- right_value: bfloat16 [8, 1024, 256], P('rows', 'cols'), parts along dimension 0, may hold values from -6 to 6
- bound: int32 [8], P('rows'), parts along dimension 0, may hold values from 0 to 7
Outputs:
- left_out: bfloat16 [8, 1024, 256], P('rows', 'cols'), parts along dimension 0
- right_out: bfloat16 [8, 1024, 256], P('rows', 'cols'), parts along dimension 0
The draws below stay inside these ranges and needn't reach their ends.
There are 4 independent parts, one for each index of `rows`. The reference program is written for one: setup_inputs(seed, part) draws one part's arguments, and reference() takes and returns one part's arrays. A program takes and returns all parts, laid end to end along the dimension named above; each array names one. Nothing has to cross between parts.
All inputs are finite; a program needn't handle non-finite values.
Results may differ from the reference program's by a relative error of at most 0.0045.
Values may be sent and summed in bfloat16 or wider, within the bound.
No kernel may reach another device: no remote copies, remote signals or barrier semaphores. Data moves between devices by JAX's collectives and lax.ppermute only.
A program may use at most 64 MiB of HBM per device.

```python
import math
import jax
import jax.numpy as jnp
from jax import lax

D = 256
ROWS = 2
COL_DEV = 128
W = 1024
N_COLS = 8


def draw_pair(key):
    base = jax.random.fold_in(key, 11)
    key_q, key_k = jax.random.split(base, 2)
    queries = jnp.clip(jax.random.normal(key_q, (ROWS, W, D)) * 1.7, -10.0, 10.0)
    keys = jnp.clip(jax.random.normal(key_k, (ROWS, W, D)) * 1.7, -10.0, 10.0)
    return (jnp.clip(queries, -16.0, 16.0), jnp.clip(keys, -16.0, 16.0))


def draw_left_query(key, part):
    return draw_pair(key)[0].astype(jnp.bfloat16)


def draw_right_key(key, part):
    return draw_pair(key)[1].astype(jnp.bfloat16)


def block_scale(own_key, extent, cuts, smallest, largest):
    factor_of = 1.0
    for position, blocks in cuts:
        draws = jax.random.uniform(jax.random.fold_in(jax.random.fold_in(own_key, 6), position), (blocks,), jnp.float32, smallest / len(cuts), largest / len(cuts))
        factor_of = factor_of * jnp.repeat(jnp.exp(draws), extent[position] // blocks).reshape((-1,) + (1,) * (len(extent) - 1 - position))
    return factor_of


def bell_draw(stream_key, dims, spread, limit, cuts=(), held_as=jnp.bfloat16):
    values = jax.random.normal(stream_key, dims, jnp.float32) * spread
    if len(cuts) > 0:
        values = block_scale(stream_key, dims, cuts, -0.22, 0.18) * values
    return jnp.clip(values, min=-limit, max=limit).astype(held_as)


def setup_inputs(seed: int = 0, part: int = 0) -> dict:
    arg_keys = jax.random.split(jax.random.key(seed), 6)
    part_keys = jax.random.split(jax.random.fold_in(arg_keys[5], part), 6)
    left_query = draw_left_query(jax.random.fold_in(jax.random.fold_in(arg_keys[5], part), 71), part)
    left_value = bell_draw(part_keys[1], (ROWS, W, D), 1.0, 6.0, ((1, 8),))
    right_key = draw_right_key(jax.random.fold_in(jax.random.fold_in(arg_keys[5], part), 71), part)
    right_value = bell_draw(part_keys[3], (ROWS, W, D), 1.0, 6.0, ((1, 8),))
    bound = jax.random.randint(part_keys[4], (ROWS,), 0, N_COLS).astype(jnp.int32)
    return {"left_query": left_query, "left_value": left_value, "right_key": right_key, "right_value": right_value, "bound": bound}


def attend_view(own, others, other_values, bound, lower_side):
    block = math.gcd(512, W)
    count = W // block
    pieces = jnp.transpose(own.reshape(ROWS, count, block, D), (1, 0, 2, 3))
    other_pos = jnp.arange(W, dtype=jnp.int32)
    reach = bound[:, None, None]
    scale = 1.0 / math.sqrt(D)

    def one_block(index_and_piece):
        index, piece = index_and_piece
        scores = jnp.einsum('rqd,rkd->rqk', piece.astype(jnp.float32), others.astype(jnp.float32)) * scale
        own_pos = index * block + jnp.arange(block, dtype=jnp.int32)
        if lower_side:
            valid = (other_pos[None, None, :] <= own_pos[None, :, None]) & ((own_pos // COL_DEV)[None, :, None] - (other_pos // COL_DEV)[None, None, :] <= reach)
        else:
            valid = (other_pos[None, None, :] >= own_pos[None, :, None]) & ((other_pos // COL_DEV)[None, None, :] - (own_pos // COL_DEV)[None, :, None] <= reach)
        top = lax.optimization_barrier(jnp.max(jnp.where(valid, scores, -1e+30), axis=-1, keepdims=True))
        weights = jnp.where(valid, jnp.exp(scores - top), 0.0)
        total = lax.optimization_barrier(jnp.sum(weights, axis=-1))
        rounded = weights.astype(jnp.bfloat16).astype(jnp.float32)
        summed = jnp.einsum('rqk,rkd->rqd', rounded, other_values.astype(jnp.float32))
        return (summed / total[:, :, None]).astype(jnp.bfloat16)
    outs = lax.map(one_block, (jnp.arange(count, dtype=jnp.int32), pieces))
    return jnp.transpose(outs, (1, 0, 2, 3)).reshape(ROWS, W, D)

def reference(left_query, left_value, right_key, right_value, bound):
    left_out = attend_view(left_query, right_key, right_value, bound, True)
    right_out = attend_view(right_key, left_query, left_value, bound, False)
    return (left_out, right_out)
```

```python
import functools
import math

import jax
import jax.numpy as jnp
from jax import lax
from jax.experimental import pallas as pl
from jax.experimental.pallas import tpu as pltpu
from jax.sharding import PartitionSpec as P

LOW = -1e30


def attend_kernel(count, scale, here_ref, bound_ref, q_ref, lv_ref, k_ref, rv_ref, *rest):
    pieces = rest[:count]
    left_ref, right_ref, mine, top, total, acc = rest[count:]
    rows_n, width, _ = q_ref.shape
    here = here_ref[0]

    def scores(a, b):
        return lax.dot_general(a, b, (((1,), (1,)), ((), ())), preferred_element_type=jnp.float32) * scale

    lane = lax.broadcasted_iota(jnp.int32, (width, width), 1)
    sub = lax.broadcasted_iota(jnp.int32, (width, width), 0)
    for side, (a_ref, b_ref, v_ref) in enumerate(((q_ref, k_ref, rv_ref), (k_ref, q_ref, lv_ref))):
        valid = (lane <= sub) if side == 0 else (lane >= sub)
        for r in range(rows_n):
            mine[side, r] = a_ref[r]
            s = jnp.where(valid, scores(a_ref[r], b_ref[r]), LOW)
            m = jnp.max(s, axis=-1, keepdims=True)
            w = jnp.exp(s - m)
            top[side, r] = m
            total[side, r] = jnp.sum(w, axis=-1, keepdims=True)
            acc[side, r] = jnp.dot(w.astype(jnp.bfloat16), v_ref[r], preferred_element_type=jnp.float32)

    for e, piece in enumerate(pieces, 1):
        other = here ^ e
        side = (other > here).astype(jnp.int32)
        distance = jnp.abs(other - here)
        for r in range(rows_n):

            @pl.when(distance <= bound_ref[r])
            def _():
                s = scores(mine[side, r], piece[0, r])
                old = top[side, r]
                m = jnp.maximum(old, jnp.max(s, axis=-1, keepdims=True))
                w = jnp.exp(s - m)
                factor = jnp.exp(old - m)
                top[side, r] = m
                total[side, r] = total[side, r] * factor + jnp.sum(w, axis=-1, keepdims=True)
                acc[side, r] = acc[side, r] * factor + jnp.dot(
                    w.astype(jnp.bfloat16), piece[1, r], preferred_element_type=jnp.float32
                )

    for side, out in enumerate((left_ref, right_ref)):
        for r in range(rows_n):
            out[r] = (acc[side, r] / total[side, r]).astype(out.dtype)


def body(left_query, left_value, right_key, right_value, bound):
    rows_n, width, depth = left_query.shape
    ncols = lax.axis_size("cols")
    here = lax.axis_index("cols")
    scale = 1.0 / math.sqrt(depth)

    def swap(value, e):
        return lax.ppermute(value, "cols", [(i, i ^ e) for i in range(ncols)])

    def outgoing(e):
        up = (here ^ e) > here
        return jnp.stack((jnp.where(up, right_key, left_query), jnp.where(up, right_value, left_value)))

    pieces = {1: swap(outgoing(1), 1)}
    for e in range(2, ncols, 2):
        pieces[e] = swap(outgoing(e), e)
    for e in range(2, ncols, 2):
        pieces[e + 1] = swap(pieces[e], 1)
    pieces = [pieces[e] for e in range(1, ncols)]

    smem = pl.BlockSpec(memory_space=pltpu.SMEM)
    vmem = pl.BlockSpec(memory_space=pltpu.VMEM)
    out = jax.ShapeDtypeStruct((rows_n, width, depth), jnp.bfloat16)
    return pl.pallas_call(
        functools.partial(attend_kernel, len(pieces), scale),
        out_shape=(out, out),
        in_specs=[smem, smem] + [vmem] * (4 + len(pieces)),
        out_specs=(vmem, vmem),
        scratch_shapes=[
            pltpu.VMEM((2, rows_n, width, depth), jnp.bfloat16),
            pltpu.VMEM((2, rows_n, width, 1), jnp.float32),
            pltpu.VMEM((2, rows_n, width, 1), jnp.float32),
            pltpu.VMEM((2, rows_n, width, depth), jnp.float32),
        ],
    )(here[None], bound, left_query, left_value, right_key, right_value, *pieces)


def solution(mesh):
    spec = P("rows", "cols", None)
    return jax.shard_map(
        body,
        mesh=mesh,
        in_specs=(spec, spec, spec, spec, P("rows")),
        out_specs=(spec, spec),
        check_vma=False,
    )
```

```python
import functools
import math

import jax
import jax.numpy as jnp
from jax import lax
from jax.experimental import pallas as pl
from jax.experimental.pallas import tpu as pltpu
from jax.sharding import PartitionSpec as P


LOW = -1e30
SMEM = pl.BlockSpec(memory_space=pltpu.SMEM)
VMEM = pl.BlockSpec(memory_space=pltpu.VMEM)


def scores(a, b, scale):
    return lax.dot_general(a, b, (((1,), (1,)), ((), ())), preferred_element_type=jnp.float32) * scale


def weighted(w, v):
    return jnp.dot(w.astype(jnp.bfloat16), v, preferred_element_type=jnp.float32)


def own_kernel(scale, bound_ref, q_ref, lv_ref, k_ref, rv_ref, mine, top, total, acc, bias):
    rows_n, width, _ = q_ref.shape
    here = lax.axis_index("cols")
    lane = lax.broadcasted_iota(jnp.int32, (width, width), 1)
    sub = lax.broadcasted_iota(jnp.int32, (width, width), 0)
    for other in range(bias.shape[0]):
        for r in range(rows_n):
            allowed = jnp.abs(other - here) <= bound_ref[r]
            bias[other, r] = jnp.full((1, width), jnp.where(allowed, 0.0, LOW), jnp.float32)
    for side, (a_ref, b_ref, v_ref) in enumerate(((q_ref, k_ref, rv_ref), (k_ref, q_ref, lv_ref))):
        valid = (lane <= sub) if side == 0 else (lane >= sub)
        for r in range(rows_n):
            mine[side, r] = a_ref[r]
            s = jnp.where(valid, scores(a_ref[r], b_ref[r], scale), LOW)
            m = jnp.max(s, axis=-1, keepdims=True)
            w = jnp.exp(s - m)
            top[side, r] = m
            total[side, r] = jnp.sum(w, axis=-1, keepdims=True)
            acc[side, r] = weighted(w, v_ref[r])


def source(even_step, odd_step):
    here = lax.axis_index("cols")
    return here ^ jnp.where(here % 2 == 1, odd_step, even_step)


def fold(scale, bias, mine, state, new_state, group):
    top, total, acc = state
    new_top, new_total, new_acc = new_state
    others = [source(*steps) for _, steps in group]
    side = (others[0] > lax.axis_index("cols")).astype(jnp.int32)
    for r in range(mine.shape[1]):
        own = mine[side, r]
        parts = [
            scores(own, piece[0, r], scale) + bias[other, r]
            for (piece, _), other in zip(group, others)
        ]
        old = top[side, r]
        m = old
        for s in parts:
            m = jnp.maximum(m, jnp.max(s, axis=-1, keepdims=True))
        factor = jnp.exp(old - m)
        summed = total[side, r] * factor
        product = acc[side, r] * factor
        for s, (piece, _) in zip(parts, group):
            w = jnp.exp(s - m)
            summed = summed + jnp.sum(w, axis=-1, keepdims=True)
            product = product + weighted(w, piece[1, r])
        new_top[side, r] = m
        new_total[side, r] = summed
        new_acc[side, r] = product


def fold_kernel(steps, scale, bias, mine, top, total, acc, *rest):
    pieces, outs = rest[: len(steps)], rest[len(steps) :]
    fold(scale, bias, mine, (top, total, acc), outs, list(zip(pieces, steps)))


def last_kernel(steps, scale, bias, mine, top, total, acc, *rest):
    pieces, (left_ref, right_ref) = rest[: len(steps)], rest[len(steps) :]
    state = (top, total, acc)
    fold(scale, bias, mine, state, state, list(zip(pieces, steps)))
    for side, out in enumerate((left_ref, right_ref)):
        for r in range(out.shape[0]):
            out[r] = (acc[side, r] / total[side, r]).astype(out.dtype)


def steps_of(ncols):
    chips = ncols // 2
    steps = []
    for d in range(1, chips - 1, 2):
        steps += [(2 * d, 2 * d + 2), (2 * d + 2, 2 * d)]
    return steps + [(2 * chips - 2, 2 * chips - 2)] * (chips % 2 == 0 and chips > 1)


def body(left_query, left_value, right_key, right_value, bound):
    rows_n, width, depth = left_query.shape
    ncols = lax.axis_size("cols")
    here = lax.axis_index("cols")
    scale = 1.0 / math.sqrt(depth)

    def move(value, step):
        pairs = [(i, i ^ step[i % 2]) for i in range(ncols)]
        return lax.ppermute(value, "cols", pairs)

    def outgoing(step):
        up = source(*step) > here
        return jnp.stack((jnp.where(up, right_key, left_query), jnp.where(up, right_value, left_value)))

    steps = steps_of(ncols)
    near = [(move(outgoing(s), s), s) for s in steps]
    partner = move(outgoing((1, 1)), (1, 1))
    far = [(move(piece, (1, 1)), (s[1] ^ 1, s[0] ^ 1)) for piece, s in near]

    params = pltpu.CompilerParams(vmem_limit_bytes=16 * 1024 * 1024)
    flops = 4 * rows_n * width * width * depth
    state_shape = [
        jax.ShapeDtypeStruct((2, rows_n, width, 1), jnp.float32),
        jax.ShapeDtypeStruct((2, rows_n, width, 1), jnp.float32),
        jax.ShapeDtypeStruct((2, rows_n, width, depth), jnp.float32),
    ]
    mine, *state, bias = pl.pallas_call(
        functools.partial(own_kernel, scale),
        out_shape=[
            jax.ShapeDtypeStruct((2, rows_n, width, depth), jnp.bfloat16),
            *state_shape,
            jax.ShapeDtypeStruct((ncols, rows_n, 1, width), jnp.float32),
        ],
        in_specs=[SMEM] + [VMEM] * 4,
        out_specs=[VMEM] * 5,
        compiler_params=params,
        name="own",
    )(bound, left_query, left_value, right_key, right_value)

    def run(kernel, group, out_shape, aliases):
        pieces, offsets = zip(*group)
        return pl.pallas_call(
            functools.partial(kernel, offsets, scale),
            out_shape=out_shape,
            in_specs=[VMEM] * (5 + len(pieces)),
            out_specs=[VMEM] * len(out_shape),
            input_output_aliases=aliases,
            compiler_params=params,
            cost_estimate=pl.CostEstimate(
                flops=flops * len(pieces), bytes_accessed=(len(pieces) + 4) * 2**18, transcendentals=0
            ),
        )(bias, mine, *state, *pieces)

    groups = [[(partner, (1, 1))]]
    for i in range(0, len(steps) - 1, 2):
        groups += [[near[i], far[i + 1]], [near[i + 1], far[i]]]
    for group in groups:
        state = run(fold_kernel, group, state_shape, {2: 0, 3: 1, 4: 2})
    out = jax.ShapeDtypeStruct((rows_n, width, depth), jnp.bfloat16)
    return tuple(run(last_kernel, [near[-1], far[-1]], [out, out], {}))


def solution(mesh):
    spec = P("rows", "cols", None)

    return jax.shard_map(
        body,
        mesh=mesh,
        in_specs=(spec, spec, spec, spec, P("rows")),
        out_specs=(spec, spec),
        check_vma=False,
    )
```

```python
import functools
import math

import jax
import jax.numpy as jnp
from jax import lax
from jax.experimental import pallas as pl
from jax.experimental.pallas import tpu as pltpu
from jax.sharding import PartitionSpec as P


LOW = -1e30
SMEM = pl.BlockSpec(memory_space=pltpu.SMEM)
VMEM = pl.BlockSpec(memory_space=pltpu.VMEM)


def scores(a, b, scale):
    return lax.dot_general(a, b, (((1,), (1,)), ((), ())), preferred_element_type=jnp.float32) * scale


def weighted(w, v):
    return jnp.dot(w.astype(jnp.bfloat16), v, preferred_element_type=jnp.float32)


def own_kernel(scale, bound_ref, q_ref, lv_ref, k_ref, rv_ref, mine, top, total, acc, bias):
    rows_n, width, _ = q_ref.shape
    here = lax.axis_index("cols")
    lane = lax.broadcasted_iota(jnp.int32, (width, width), 1)
    sub = lax.broadcasted_iota(jnp.int32, (width, width), 0)
    for other in range(bias.shape[0]):
        for r in range(rows_n):
            allowed = jnp.abs(other - here) <= bound_ref[r]
            bias[other, r] = jnp.full((1, width), jnp.where(allowed, 0.0, LOW), jnp.float32)
    for side, (a_ref, b_ref, v_ref) in enumerate(((q_ref, k_ref, rv_ref), (k_ref, q_ref, lv_ref))):
        valid = (lane <= sub) if side == 0 else (lane >= sub)
        for r in range(rows_n):
            mine[side, r] = a_ref[r]
            s = jnp.where(valid, scores(a_ref[r], b_ref[r], scale), LOW)
            m = jnp.broadcast_to(jnp.max(s, axis=-1, keepdims=True), s.shape)
            w = jnp.exp(s - m)
            top[side, r] = m
            total[side, r] = w
            acc[side, r] = weighted(w, v_ref[r])


def source(even_step, odd_step):
    here = lax.axis_index("cols")
    return here ^ jnp.where(here % 2 == 1, odd_step, even_step)


def fold(scale, bias, mine, state, new_state, group):
    top, total, acc = state
    new_top, new_total, new_acc = new_state
    others = [source(*steps) for _, steps in group]
    side = (others[0] > lax.axis_index("cols")).astype(jnp.int32)
    for r in range(mine.shape[1]):
        own = mine[side, r]
        parts = [
            scores(own, piece[0, r], scale) + bias[other, r]
            for (piece, _), other in zip(group, others)
        ]
        old = top[side, r]
        peak = functools.reduce(jnp.maximum, parts)
        m = jnp.maximum(old, jnp.max(peak, axis=-1, keepdims=True))
        factor = jnp.exp(old - m)
        summed = total[side, r] * factor
        product = acc[side, r] * jnp.concatenate([factor] * (acc.shape[-1] // factor.shape[-1]), axis=-1)
        for s, (piece, _) in zip(parts, group):
            w = jnp.exp(s - m)
            summed = summed + w
            product = product + weighted(w, piece[1, r])
        new_top[side, r] = m
        new_total[side, r] = summed
        new_acc[side, r] = product


def fold_kernel(steps, scale, bias, mine, top, total, acc, *rest):
    pieces, outs = rest[: len(steps)], rest[len(steps) :]
    fold(scale, bias, mine, (top, total, acc), outs, list(zip(pieces, steps)))


def last_kernel(steps, scale, bias, mine, top, total, acc, *rest):
    pieces, (left_ref, right_ref) = rest[: len(steps)], rest[len(steps) :]
    state = (top, total, acc)
    fold(scale, bias, mine, state, state, list(zip(pieces, steps)))
    for side, out in enumerate((left_ref, right_ref)):
        for r in range(out.shape[0]):
            inverse = 1.0 / jnp.sum(total[side, r], axis=-1, keepdims=True)
            out[r] = (acc[side, r] * inverse).astype(out.dtype)


def steps_of(ncols):
    chips = ncols // 2
    steps = []
    for d in range(1, chips - 1, 2):
        steps += [(2 * d, 2 * d + 2), (2 * d + 2, 2 * d)]
    return steps + [(2 * chips - 2, 2 * chips - 2)] * (chips % 2 == 0 and chips > 1)


def body(left_query, left_value, right_key, right_value, bound):
    rows_n, width, depth = left_query.shape
    ncols = lax.axis_size("cols")
    scale = 1.0 / math.sqrt(depth)

    def move(value, step):
        pairs = [(i, i ^ step[i % 2]) for i in range(ncols)]
        return lax.ppermute(value, "cols", pairs)

    def outgoing(step):
        up = source(*step) > lax.axis_index("cols")
        return jnp.stack((jnp.where(up, right_key, left_query), jnp.where(up, right_value, left_value)))

    params = pltpu.CompilerParams(vmem_limit_bytes=16 * 1024 * 1024)
    steps = steps_of(ncols)
    near = [(move(outgoing(s), s), s) for s in steps]
    partner = move(outgoing((1, 1)), (1, 1))
    far = [(move(piece, (1, 1)), (s[1] ^ 1, s[0] ^ 1)) for piece, s in near]

    flops = 4 * rows_n * width * width * depth
    state_shape = [
        jax.ShapeDtypeStruct((2, rows_n, width, width), jnp.float32),
        jax.ShapeDtypeStruct((2, rows_n, width, width), jnp.float32),
        jax.ShapeDtypeStruct((2, rows_n, width, depth), jnp.float32),
    ]
    mine, *state, bias = pl.pallas_call(
        functools.partial(own_kernel, scale),
        out_shape=[
            jax.ShapeDtypeStruct((2, rows_n, width, depth), jnp.bfloat16),
            *state_shape,
            jax.ShapeDtypeStruct((ncols, rows_n, 1, width), jnp.float32),
        ],
        in_specs=[SMEM] + [VMEM] * 4,
        out_specs=[VMEM] * 5,
        compiler_params=params,
        name="own",
    )(bound, left_query, left_value, right_key, right_value)

    def run(kernel, group, out_shape, aliases):
        pieces, offsets = zip(*group)
        return pl.pallas_call(
            functools.partial(kernel, offsets, scale),
            out_shape=out_shape,
            in_specs=[VMEM] * (5 + len(pieces)),
            out_specs=[VMEM] * len(out_shape),
            input_output_aliases=aliases,
            compiler_params=params,
            cost_estimate=pl.CostEstimate(
                flops=flops * len(pieces), bytes_accessed=(len(pieces) + 4) * 2**18, transcendentals=0
            ),
        )(bias, mine, *state, *pieces)

    groups = [[(partner, (1, 1))]]
    for i in range(0, len(steps) - 1, 2):
        groups += [[near[i], far[i + 1]], [near[i + 1], far[i]]]
    groups += [[near[-1]]]
    for group in groups:
        state = run(fold_kernel, group, state_shape, {2: 0, 3: 1, 4: 2})
    out = jax.ShapeDtypeStruct((rows_n, width, depth), jnp.bfloat16)
    return tuple(run(last_kernel, [far[-1]], [out, out], {}))


def solution(mesh):
    spec = P("rows", "cols", None)

    return jax.shard_map(
        body,
        mesh=mesh,
        in_specs=(spec, spec, spec, spec, P("rows")),
        out_specs=(spec, spec),
        check_vma=False,
    )
```
